32 devices in a mesh: groups: 2 (over x), roll: 8 (over z, y), width: 2 (over core).
Axes of the slice: x: 2, y: 2, z: 4, core: 2. Of those that a mesh axis runs over, the one named last changes fastest.
Arguments:
- lines_y: bfloat16 [1792, 16384], P(('groups', 'roll'), 'width'), parts along dimension 0, may hold values from -96 to 96
- defect_mask: int32 [1792, 128], P(('groups', 'roll'), 'width'), parts along dimension 0, may hold values from 0 to 1
- loading: bfloat16 [16384, 128], P('width'), may hold values from -17 to 17
- decay_rate: float32 [64], replicated, may hold values from 1e-05 to 0.03
- angle: float32 [64], replicated, may hold values from -3.140625 to 3.140625
- gain: float32 [64], replicated, may hold values from 0.0003 to 0.009
- smooth_gain: float32 [64], replicated, may hold values from 0.3 to 0.9998
- initial: float32 [256], P('groups'), parts along dimension 0, may hold values from -4 to 4
Outputs:
- smoothed: float32 [1792, 128], P(('groups', 'roll')), parts along dimension 0
- background: bfloat16 [1792, 16384], P(('groups', 'roll'), 'width'), parts along dimension 0
The draws below stay inside these ranges and needn't reach their ends.
There are 2 independent parts, one for each index of `groups`. The reference program is written for one: setup_inputs(seed, part) draws one part's arguments, and reference() takes and returns one part's arrays. A program takes and returns all parts, laid end to end along the dimension named above; an argument that names none is the same for every part. Nothing has to cross between parts.
All inputs are finite; a program needn't handle non-finite values.
Results may differ from the reference program's by a relative error of at most 0.0049.
Values sent between devices are 32-bit elements; how exact they have to be, the bound alone decides.
A program may use at most 64 MiB of HBM per device.

```python
import math
import jax
import jax.numpy as jnp
from jax import lax

S = 128
P_SIZE = 16384
PIX_BLK = 128
LINES_DEV = 112
HALF = 64
NBLK = 128
LINES = 896
N_ROLL = 8


def draw_defect_mask(key, part):
    key_rate = jax.random.fold_in(key, 11)
    key_cell = jax.random.fold_in(key, 12)
    rates = jax.random.randint(key_rate, (LINES, 1), 1, 9)
    cells = jax.random.randint(key_cell, (LINES, NBLK), 0, 8)
    return jnp.where(cells < rates, 1, 0).astype(jnp.int32)


def draw_loading(key, part):
    key_scale = jax.random.fold_in(key, 21)
    key_dir = jax.random.fold_in(key, 22)
    key_noise = jax.random.fold_in(key, 23)
    key_weight = jax.random.fold_in(key, 24)
    spread = jnp.exp(jax.random.uniform(key_scale, (NBLK, 1, 1), jnp.float32, math.log(0.5), math.log(1.6)))
    direction = jax.random.truncated_normal(key_dir, -3.0, 3.0, (NBLK, 1, S), jnp.float32) * 0.7
    noise = jax.random.truncated_normal(key_noise, -4.0, 4.0, (NBLK, PIX_BLK, S), jnp.float32)
    weight = jax.random.truncated_normal(key_weight, -3.0, 3.0, (NBLK, PIX_BLK, 1), jnp.float32)
    full = spread * (noise + weight * direction)
    return full.reshape(P_SIZE, S).astype(jnp.bfloat16)


def draw_smooth_gain(key, part):
    key_pick = jax.random.fold_in(key, 31)
    key_slow = jax.random.fold_in(key, 32)
    key_fast = jax.random.fold_in(key, 33)
    order = jax.random.permutation(key_pick, HALF)
    slow_vals = jax.random.uniform(key_slow, (HALF,), jnp.float32, 0.9994, 0.9998)
    fast_vals = jax.random.uniform(key_fast, (HALF,), jnp.float32, 0.3, 0.95)
    slow_count = HALF // 2
    return jnp.where(order < slow_count, slow_vals, fast_vals).astype(jnp.float32)


def level_of(stream_key, extent, shards, least, top_value):
    loudness = 1.0
    for axis_at, blocks in shards:
        heights = jax.random.uniform(jax.random.fold_in(jax.random.fold_in(stream_key, 6), axis_at), (blocks,), jnp.float32, least / len(shards), top_value / len(shards))
        loudness = loudness * jnp.repeat(jnp.exp(heights), extent[axis_at] // blocks).reshape((-1,) + (1,) * (len(extent) - 1 - axis_at))
    return loudness


def normal_values(rng, extent, scale, most, shards=(), dtype=jnp.bfloat16):
    entries = jax.random.normal(rng, extent, jnp.float32) * scale
    if len(shards) > 0:
        entries = level_of(rng, extent, shards, -0.22, 0.18) * entries
    return jnp.clip(entries, min=-most, max=most).astype(dtype)


def setup_inputs(seed: int = 0, part: int = 0) -> dict:
    seeds = jax.random.split(jax.random.key(seed), 9)
    own_keys = jax.random.split(jax.random.fold_in(seeds[8], part), 9)
    return {
        "lines_y": normal_values(own_keys[0], (LINES, P_SIZE), 16.0, 96.0, ((0, 8), (1, 2))),
        "defect_mask": draw_defect_mask(jax.random.fold_in(jax.random.fold_in(seeds[8], part), 71), part),
        "loading": draw_loading(jax.random.fold_in(seeds[8], 71), part),
        "decay_rate": jnp.clip(jnp.exp(jax.random.uniform(seeds[3], (HALF,), jnp.float32, math.log(9.999999747378752e-06), math.log(0.03))), 9.999999747378752e-06, 0.03),
        "angle": jnp.clip(jax.random.uniform(seeds[4], (HALF,), jnp.float32, -3.140625, 3.140625), -3.140625, 3.140625),
        "gain": jnp.clip(jnp.exp(jax.random.uniform(seeds[5], (HALF,), jnp.float32, math.log(0.0003), math.log(0.009))), 0.0003, 0.009),
        "smooth_gain": draw_smooth_gain(jax.random.fold_in(seeds[8], 71), part),
        "initial": normal_values(own_keys[7], (S,), 1.0, 4.0, (), jnp.float32),
    }


def reference(lines_y, defect_mask, loading, decay_rate, angle, gain, smooth_gain, initial):
    precise_mode = lax.Precision.HIGHEST
    radius = 1.0 - decay_rate
    cos_part = radius * jnp.cos(angle)
    sin_part = radius * jnp.sin(angle)
    gain_full = jnp.concatenate([gain, gain])
    keep_part = 1.0 - smooth_gain * radius * radius
    keep_full = jnp.concatenate([keep_part, keep_part])
    load_f = loading.astype(jnp.float32).reshape(NBLK, PIX_BLK, S)
    block_gram = jnp.einsum('bps,bpt->bst', load_f, load_f, precision=precise_mode).reshape(NBLK, S * S)
    mask_rep = jnp.repeat(defect_mask.astype(jnp.bfloat16), PIX_BLK, axis=1)
    masked = lines_y * mask_rep
    projected = jnp.dot(masked, loading, preferred_element_type=jnp.float32) * (math.sqrt(S) / P_SIZE)
    mask_f = defect_mask.astype(jnp.float32)

    def advance(state, inputs):
        gram_row, proj_row = inputs
        gram_mat = gram_row.reshape(S, S)
        upper = state[:HALF]
        lower = state[HALF:]
        moved = jnp.concatenate([cos_part * upper - sin_part * lower, sin_part * upper + cos_part * lower])
        nxt = moved - gain_full * jnp.dot(gram_mat, moved, precision=precise_mode) + gain_full * proj_row
        return (nxt, nxt)

    def block_step(state, inputs):
        mask_blk, proj_blk = inputs
        grams = jnp.dot(mask_blk, block_gram, precision=precise_mode) / P_SIZE
        return lax.scan(advance, state, (grams, proj_blk))
    _, filtered = lax.scan(block_step, initial, (mask_f.reshape(N_ROLL, LINES_DEV, NBLK), projected.reshape(N_ROLL, LINES_DEV, S)))
    filtered = filtered.reshape(LINES, S)

    def retreat(state, filt_row):
        real_in = state[:HALF]
        imag_in = state[HALF:]
        real_out = smooth_gain * (cos_part * real_in + sin_part * imag_in)
        imag_out = smooth_gain * (cos_part * imag_in - sin_part * real_in)
        nxt = jnp.concatenate([real_out, imag_out]) + keep_full * filt_row
        return (nxt, nxt)
    _, earlier = lax.scan(retreat, filtered[LINES - 1], filtered[:LINES - 1], reverse=True)
    smoothed = jnp.concatenate([earlier, filtered[LINES - 1:]], axis=0)
    background = (jnp.dot(smoothed.astype(jnp.bfloat16), loading.T, preferred_element_type=jnp.float32) * (1.0 / math.sqrt(S))).astype(jnp.bfloat16)
    return (smoothed, background)
```

```python
import functools
import math

import jax
import jax.numpy as jnp
from jax import lax
from jax.experimental import pallas as pl
from jax.experimental.pallas import tpu as pltpu
from jax.sharding import PartitionSpec as P

PIX_BLK = 128
CHAINS = 8
PIECES = 8
MESH = pl.DeviceIdType.MESH
HI = lax.Precision.HIGHEST
F32 = jnp.float32
BF16 = jnp.bfloat16


def turn(v):
    return pltpu.roll(v, v.shape[-1] // 2, 1)


def join(first, second, dst):
    s = second.shape[1]
    r = jnp.dot(first, second[:s], precision=HI, preferred_element_type=F32)
    dst[0:s, :] = r[:s]
    dst[s : s + 8, :] = r[s:] + second[s:]


def column(x):
    return jnp.broadcast_to(x, (x.shape[1], x.shape[1])).T


def apply(xcol, m):
    s = xcol.shape[0]
    return jnp.sum(m[:s] * xcol, axis=0, keepdims=True) + m[s : s + 1]


def powers(fr, fi, expo, bits):
    tr = jnp.ones(expo.shape, F32)
    ti = jnp.zeros(expo.shape, F32)
    for k in range(bits):
        on = (expo >> k) & 1 == 1
        nr = tr * fr - ti * fi
        ni = tr * fi + ti * fr
        tr = jnp.where(on, nr, tr)
        ti = jnp.where(on, ni, ti)
        fr, fi = fr * fr - fi * fi, 2.0 * fr * fi
    return tr, ti


def kernel(
    n_roll, y_ref, mask_ref, load_ref, par_ref, init_ref, out_ref,
    bs, gsend, gown, grecv, pacc, precv, pown, pall, comb, mcore, mpair, mquad, mrecv, xs,
    xsend, xrecv, bsend, brecv, ssend, srecv,
    g_ss, g_rs, one_ss, one_rs, b_ss, b_rs,
):
    s = load_ref.shape[1]
    lines = y_ref.shape[0]
    th = lines // 2
    steps = th // CHAINS
    nb = load_ref.shape[0] // PIX_BLK
    nq = 2 * n_roll
    r = lax.axis_index("roll")
    w = lax.axis_index("width")
    q = 2 * r + w
    other = 1 - w

    def at(place):
        return {"roll": lax.div(place, 2), "width": lax.rem(place, 2)}

    barrier = pltpu.get_barrier_semaphore()

    def greet(d, _):
        pl.semaphore_signal(barrier, inc=1, device_id=at(lax.rem(q + d, nq)), device_id_type=MESH)
        return 0

    lax.fori_loop(1, nq, greet, 0)

    cosd = par_ref[0:1, :]
    sind = par_ref[1:2, :]
    kap_g = par_ref[2:3, :]
    kap_p = par_ref[3:4, :]
    fr = par_ref[4:5, :]
    fi = par_ref[5:6, :]
    keep = par_ref[6:7, :]
    sgn = par_ref[7:8, :]

    own_rows = pl.ds(pl.multiple_of(w * th, 8), th)
    oth_rows = pl.ds(pl.multiple_of(other * th, 8), th)
    m_all = mask_ref[...].astype(F32).astype(BF16)
    m_two = jnp.concatenate(
        [mask_ref[oth_rows, :].astype(F32), mask_ref[own_rows, :].astype(F32)], axis=0
    ).astype(BF16)

    pacc[...] = jnp.zeros_like(pacc)
    per = 4

    def blocks(g, _):
        total = pacc[...]
        for k in range(per):
            b = g * per + k
            rows = pl.ds(pl.multiple_of(b * PIX_BLK, PIX_BLK), PIX_BLK)
            h = load_ref[rows, :]
            bs[pl.ds(pl.multiple_of(b * s, s), s), :] = lax.dot_general(
                h, h, (((0,), (0,)), ((), ())), preferred_element_type=F32
            )
            pick = jnp.where(lax.broadcasted_iota(jnp.int32, (nb, PIX_BLK), 0) == b, 1.0, 0.0).astype(BF16)
            mb = jnp.dot(m_all, pick, preferred_element_type=F32)
            my = (y_ref[:, rows].astype(F32) * mb).astype(BF16)
            total += jnp.dot(my, h, preferred_element_type=F32)
        pacc[...] = total
        return 0

    lax.fori_loop(0, nb // per, blocks, 0)

    pl.semaphore_wait(barrier, nq - 1)

    def exchange(src, dst, k, dev):
        return pltpu.make_async_remote_copy(
            src_ref=src, dst_ref=dst, send_sem=one_ss.at[k], recv_sem=one_rs.at[k],
            device_id=dev, device_id_type=MESH,
        )

    partner = {"roll": r, "width": other}
    c_proj = exchange(pacc.at[oth_rows, :], precv, 0, partner)
    c_proj.start()

    piece = s // PIECES
    copies = []
    for c in range(PIECES):
        def rows_of(g, _):
            for k in range(per):
                i = c * piece + g * per + k
                bi = bs[pl.ds(i, nb, stride=s), :].astype(BF16)
                res = jnp.dot(m_two, bi, preferred_element_type=F32)
                dst = pl.ds(pl.multiple_of(i * th, 8), th)
                gsend[dst, :] = res[:th]
                gown[dst, :] = res[th:]
            return 0

        lax.fori_loop(0, piece // per, rows_of, 0)
        span = pl.ds(c * piece * th, piece * th)
        cp = pltpu.make_async_remote_copy(
            src_ref=gsend.at[span, :], dst_ref=grecv.at[span, :], send_sem=g_ss.at[c],
            recv_sem=g_rs.at[c], device_id=partner, device_id_type=MESH,
        )
        cp.start()
        copies.append(cp)

    row_t = lax.broadcasted_iota(jnp.int32, (th, s), 0)
    tail_r, tail_i = powers(fr, fi, th - row_t, th.bit_length())
    far_r, far_i = powers(
        tail_r[0:1], tail_i[0:1], lax.broadcasted_iota(jnp.int32, (nq, s), 0), nq.bit_length()
    )

    ident = jnp.where(
        lax.broadcasted_iota(jnp.int32, (s + 8, s), 0) == lax.broadcasted_iota(jnp.int32, (s + 8, s), 1),
        1.0, 0.0,
    )
    for c in range(CHAINS):
        pall[c * (steps + 1)] = ident

    c_proj.wait()
    pown[...] = (pacc[own_rows, :] + precv[...]) * kap_p
    for cp in copies:
        cp.wait()

    def step(k, _):
        for c in range(CHAINS):
            t = c * steps + k
            gram = (gown[pl.ds(t, s, stride=th), :] + grecv[pl.ds(t, s, stride=th), :]).astype(BF16)
            p = pall[c * (steps + 1) + k]
            u = p * cosd + turn(p) * sind
            nxt = u - kap_g * jnp.dot(u.astype(BF16), gram, preferred_element_type=F32)
            pall[c * (steps + 1) + k + 1, 0:s, :] = nxt[:s]
            pall[c * (steps + 1) + k + 1, s : s + 8, :] = nxt[s:] + pown[pl.ds(t, 1), :]
        return 0

    lax.fori_loop(0, steps, step, 0)

    def last(c):
        return pall[c * (steps + 1) + steps]

    for p in range(4):
        join(last(2 * p), last(2 * p + 1), comb.at[p])
    join(comb[0], comb[1], comb.at[4])
    join(comb[2], comb[3], comb.at[5])
    join(comb[4], comb[5], mcore)

    c_core = exchange(mcore, mrecv.at[0], 1, partner)
    c_core.start()
    c_core.wait()
    mine = mcore[...]
    theirs = mrecv[0]
    join(jnp.where(w == 0, mine, theirs), jnp.where(w == 0, theirs, mine), mpair)

    odd = lax.rem(r, 2)
    c_pair = exchange(mpair, mrecv.at[1], 2, {"roll": r + 1 - 2 * odd, "width": w})
    c_pair.start()
    c_pair.wait()
    mine = mpair[...]
    theirs = mrecv[1]
    join(jnp.where(odd == 0, mine, theirs), jnp.where(odd == 0, theirs, mine), mquad)

    onward = lax.rem(r + 2, n_roll)
    c_x = exchange(xsend, xrecv, 3, {"roll": onward, "width": w})

    @pl.when(r < 2)
    def _():
        xrecv[...] = jnp.broadcast_to(init_ref[...], xrecv.shape)

    @pl.when(r >= 2)
    def _():
        c_x.wait_recv()

    x = xrecv[0:1, :]
    xcol = column(x)

    @pl.when(r < n_roll - 2)
    def _():
        xsend[...] = jnp.broadcast_to(apply(xcol, mquad[...]), xsend.shape)
        c_x.start()

    x = jnp.where(odd == 1, apply(xcol, mrecv[1]), x)
    x = jnp.where(w == 1, apply(column(x), mrecv[0]), x)

    def along(c, xc):
        col = column(xc)
        val = None
        for k in range(steps):
            val = apply(col, pall[c * (steps + 1) + k + 1])
            xs[c * steps + k : c * steps + k + 1, :] = val
        return col, val

    col0, x1 = along(0, x)
    x4 = apply(col0, comb[4])
    x2 = apply(col0, comb[0])
    col4, x5 = along(4, x4)
    x6 = apply(col4, comb[2])
    _, x3 = along(2, x2)
    _, x7 = along(6, x6)
    along(1, x1)
    along(3, x3)
    along(5, x5)
    along(7, x7)

    final = jnp.logical_and(q == nq - 1, row_t == th - 1)
    xf = xs[...]
    v = jnp.where(final, xf, keep * xf)
    ar, ai = fr, fi
    hop = 1
    while hop < th:
        later = jnp.where(row_t < th - hop, pltpu.roll(v, th - hop, 0), 0.0)
        v = v + later * ar + turn(later) * (ai * sgn)
        ar, ai = ar * ar - ai * ai, 2.0 * ar * ai
        hop *= 2

    bsend[...] = jnp.broadcast_to(v[0:1, :], bsend.shape)

    def away(d):
        return pltpu.make_async_remote_copy(
            src_ref=bsend, dst_ref=brecv.at[d - 1], send_sem=b_ss.at[d - 1], recv_sem=b_rs.at[d - 1],
            device_id=at(lax.rem(q - d + nq, nq)), device_id_type=MESH,
        )

    def send_b(d, _):
        @pl.when(q >= d)
        def _():
            away(d).start()

        return 0

    def recv_b(d, _):
        @pl.when(q + d < nq)
        def _():
            away(d).wait_recv()

        return 0

    def sent_b(d, _):
        @pl.when(q >= d)
        def _():
            away(d).wait_send()

        return 0

    brecv[nq - 1] = jnp.zeros(brecv.shape[1:], F32)

    def blank(d, _):
        @pl.when(q + d >= nq)
        def _():
            brecv[d - 1] = jnp.zeros(brecv.shape[1:], F32)

        return 0

    lax.fori_loop(1, nq, send_b, 0)
    lax.fori_loop(1, nq, blank, 0)
    lax.fori_loop(1, nq, recv_b, 0)
    late = brecv[:, 0, :]
    s_in = jnp.sum(late * far_r + turn(late) * (far_i * sgn), axis=0, keepdims=True)
    v = v + s_in * tail_r + turn(jnp.broadcast_to(s_in, (8, s)))[0:1] * (tail_i * sgn)
    ssend[...] = v
    c_s = exchange(ssend, srecv, 4, partner)
    c_s.start()
    out_ref[own_rows, :] = v
    c_s.wait()
    out_ref[oth_rows, :] = srecv[...]

    @pl.when(r < n_roll - 2)
    def _():
        c_x.wait_send()

    lax.fori_loop(1, nq, sent_b, 0)


def shards(n_roll, lines_y, defect_mask, loading, decay_rate, angle, gain, smooth_gain, initial):
    s = loading.shape[1]
    lines = lines_y.shape[0]
    th = lines // 2
    steps = th // CHAINS
    nb = loading.shape[0] // PIX_BLK
    nq = 2 * n_roll
    pixels = lines_y.shape[1] * lax.axis_size("width")
    radius = 1.0 - decay_rate
    cosr = radius * jnp.cos(angle)
    sinr = radius * jnp.sin(angle)
    one = jnp.ones_like(gain)
    keep = 1.0 - smooth_gain * radius * radius

    left = jnp.stack([
        cosr, -sinr, gain / pixels, gain * (math.sqrt(s) / pixels),
        smooth_gain * cosr, -(smooth_gain * sinr), keep, -one,
    ])
    right = jnp.stack([
        cosr, sinr, gain / pixels, gain * (math.sqrt(s) / pixels),
        smooth_gain * cosr, -(smooth_gain * sinr), keep, one,
    ])
    par = jnp.concatenate([left, right], axis=1)
    vm = pl.BlockSpec(memory_space=pltpu.VMEM)
    smoothed = pl.pallas_call(
        functools.partial(kernel, n_roll),
        out_shape=jax.ShapeDtypeStruct((lines, s), F32),
        in_specs=[vm] * 5,
        out_specs=vm,
        scratch_shapes=[
            pltpu.VMEM((nb * s, s), F32),
            pltpu.VMEM((s * th, s), F32),
            pltpu.VMEM((s * th, s), F32),
            pltpu.VMEM((s * th, s), F32),
            pltpu.VMEM((lines, s), F32),
            pltpu.VMEM((th, s), F32),
            pltpu.VMEM((th, s), F32),
            pltpu.VMEM((CHAINS * (steps + 1), s + 8, s), F32),
            pltpu.VMEM((6, s + 8, s), F32),
            pltpu.VMEM((s + 8, s), F32),
            pltpu.VMEM((s + 8, s), F32),
            pltpu.VMEM((s + 8, s), F32),
            pltpu.VMEM((2, s + 8, s), F32),
            pltpu.VMEM((th, s), F32),
            pltpu.VMEM((8, s), F32),
            pltpu.VMEM((8, s), F32),
            pltpu.VMEM((8, s), F32),
            pltpu.VMEM((nq, 8, s), F32),
            pltpu.VMEM((th, s), F32),
            pltpu.VMEM((th, s), F32),
            pltpu.SemaphoreType.DMA((PIECES,)),
            pltpu.SemaphoreType.DMA((PIECES,)),
            pltpu.SemaphoreType.DMA((5,)),
            pltpu.SemaphoreType.DMA((5,)),
            pltpu.SemaphoreType.DMA((nq,)),
            pltpu.SemaphoreType.DMA((nq,)),
        ],
        compiler_params=pltpu.CompilerParams(
            collective_id=0, has_side_effects=True, vmem_limit_bytes=48 * 1024 * 1024
        ),
        name="filter_smoother",
    )(lines_y, defect_mask, loading, par, initial.reshape(1, s))
    image_rows = lax.dot_general(
        smoothed.astype(BF16), loading, (((1,), (1,)), ((), ())), preferred_element_type=F32
    )
    background = (image_rows * (1.0 / math.sqrt(s))).astype(BF16)
    return (smoothed, background)


def solution(mesh):
    in_specs = (
        P(("groups", "roll"), "width"),
        P(("groups", "roll"), "width"),
        P("width", None),
        P(),
        P(),
        P(),
        P(),
        P("groups"),
    )
    out_specs = (P(("groups", "roll"), None), P(("groups", "roll"), "width"))
    return jax.shard_map(
        functools.partial(shards, mesh.shape["roll"]),
        mesh=mesh, in_specs=in_specs, out_specs=out_specs, check_vma=False,
    )
```

```python
import functools
import math

import jax
import jax.numpy as jnp
from jax import lax
from jax.experimental import pallas as pl
from jax.experimental.pallas import tpu as pltpu
from jax.sharding import PartitionSpec as P

PIX_BLK = 128
CHAINS = 8
PIECES = 8
MESH = pl.DeviceIdType.MESH
HI = lax.Precision.HIGHEST
F32 = jnp.float32
BF16 = jnp.bfloat16


def turn(v):
    return pltpu.roll(v, v.shape[-1] // 2, 1)


def join(first, second, dst):
    s = second.shape[1]
    r = jnp.dot(first, second[:s], precision=HI, preferred_element_type=F32)
    dst[0:s, :] = r[:s]
    dst[s : s + 8, :] = r[s:] + second[s:]


def column(x):
    return jnp.broadcast_to(x, (x.shape[1], x.shape[1])).T


def apply(xcol, m):
    s = xcol.shape[0]
    return jnp.sum(m[:s] * xcol, axis=0, keepdims=True) + m[s : s + 1]


def powers(fr, fi, expo, bits):
    tr = jnp.ones(expo.shape, F32)
    ti = jnp.zeros(expo.shape, F32)
    for k in range(bits):
        on = (expo >> k) & 1 == 1
        nr = tr * fr - ti * fi
        ni = tr * fi + ti * fr
        tr = jnp.where(on, nr, tr)
        ti = jnp.where(on, ni, ti)
        fr, fi = fr * fr - fi * fi, 2.0 * fr * fi
    return tr, ti


def kernel(
    n_roll, y_hbm, maskt_hbm, load_hbm, decay_hbm, angle_hbm, gain_hbm, sgain_hbm, init_hbm, out_ref,
    y_ref, load_ref, maskt_ref, par_in, init_ref,
    mfull, mrem, bs, gown, pacc, precv, pown, pall, comb, mcore, mpair, mquad, mrecv, xs,
    xsend, xrecv, bsend, bquad, brows, zsend, zrecv, ssend, srecv,
    in_s, small_s, g_ss, g_rs, one_ss, one_rs, b_ss, b_rs, z_ss, z_rs,
):
    s = load_ref.shape[1]
    half = s // 2
    lines = y_ref.shape[0]
    th = lines // 2
    steps = th // CHAINS
    nb = load_ref.shape[0] // PIX_BLK
    pixels = 2 * load_ref.shape[0]
    nq = 2 * n_roll
    nz = n_roll // 2
    r = lax.axis_index("roll")
    w = lax.axis_index("width")
    q = 2 * r + w
    other = 1 - w
    wide = load_ref.shape[0] // PIECES

    smalls = [
        pltpu.make_async_copy(src, dst, small_s.at[k])
        for k, (src, dst) in enumerate([
            (maskt_hbm, maskt_ref), (decay_hbm, par_in.at[0]), (angle_hbm, par_in.at[1]),
            (gain_hbm, par_in.at[2]), (sgain_hbm, par_in.at[3]), (init_hbm, init_ref),
        ])
    ]
    for cp in smalls:
        cp.start()
    loads = []
    for c in range(PIECES):
        span = pl.ds(c * wide, wide)
        pair = (
            pltpu.make_async_copy(load_hbm.at[span, :], load_ref.at[span, :], in_s.at[0, c]),
            pltpu.make_async_copy(y_hbm.at[:, span], y_ref.at[:, span], in_s.at[1, c]),
        )
        for cp in pair:
            cp.start()
        loads.append(pair)

    def at(place):
        return {"roll": lax.div(place, 2), "width": lax.rem(place, 2)}

    barrier = pltpu.get_barrier_semaphore()

    def greet(d, _):
        pl.semaphore_signal(barrier, inc=1, device_id=at(lax.rem(q + d, nq)), device_id_type=MESH)
        return 0

    lax.fori_loop(1, nq, greet, 0)
    for cp in smalls:
        cp.wait()

    eye = jnp.where(
        lax.broadcasted_iota(jnp.int32, (nb, nb), 0) == lax.broadcasted_iota(jnp.int32, (nb, nb), 1),
        1.0, 0.0,
    ).astype(BF16)
    m_f = lax.dot_general(
        maskt_ref[...].astype(F32).astype(BF16), eye, (((0,), (0,)), ((), ())),
        preferred_element_type=F32,
    )
    mfull[...] = m_f
    m_all = m_f.astype(BF16)

    own_rows = pl.ds(pl.multiple_of(w * th, 8), th)
    oth_rows = pl.ds(pl.multiple_of(other * th, 8), th)

    def exchange(src, dst, k, dev):
        return pltpu.make_async_remote_copy(
            src_ref=src, dst_ref=dst, send_sem=one_ss.at[k], recv_sem=one_rs.at[k],
            device_id=dev, device_id_type=MESH,
        )

    partner = {"roll": r, "width": other}
    c_mask = exchange(mfull.at[oth_rows, :], mrem, 5, partner)

    pacc[...] = jnp.zeros_like(pacc)
    per = 4
    few = nb // PIECES
    copies = []
    for c in range(PIECES):
        for cp in loads[c]:
            cp.wait()

        def blocks(g, _):
            b0 = c * few + g * per
            rows = pl.ds(pl.multiple_of(b0 * PIX_BLK, per * PIX_BLK), per * PIX_BLK)
            hh = load_ref[rows, :]
            for k in range(per):
                h = hh[k * PIX_BLK : (k + 1) * PIX_BLK]
                bs[pl.ds(pl.multiple_of((b0 + k) * s, s), s), :] = lax.dot_general(
                    h, h, (((0,), (0,)), ((), ())), preferred_element_type=F32
                )
            shape = (nb, per * PIX_BLK)
            pick = jnp.where(
                lax.broadcasted_iota(jnp.int32, shape, 0)
                == b0 + lax.broadcasted_iota(jnp.int32, shape, 1) // PIX_BLK,
                1.0, 0.0,
            ).astype(BF16)
            mb = jnp.dot(m_all, pick, preferred_element_type=F32).astype(BF16)
            pacc[...] += jnp.dot(y_ref[:, rows] * mb, hh, preferred_element_type=F32)
            return 0

        lax.fori_loop(0, few // per, blocks, 0)
        if c == 0:
            pl.semaphore_wait(barrier, nq - 1)
            c_mask.start()
        cp = pltpu.make_async_remote_copy(
            src_ref=bs.at[pl.ds(c * few * s, few * s), :],
            dst_ref=bs.at[pl.ds((nb + c * few) * s, few * s), :],
            send_sem=g_ss.at[c], recv_sem=g_rs.at[c], device_id=partner, device_id_type=MESH,
        )
        cp.start()
        copies.append(cp)

    c_proj = exchange(pacc.at[oth_rows, :], precv, 0, partner)
    c_proj.start()

    decay = par_in[0]
    angle = par_in[1]
    gain = par_in[2]
    sgain = par_in[3]
    radius = 1.0 - decay
    cosr = radius * jnp.cos(angle)
    sinr = radius * jnp.sin(angle)
    keep_h = 1.0 - sgain * radius * radius

    def both(a, b):
        return jnp.concatenate([a, b], axis=1)

    cosd = both(cosr, cosr)
    sind = both(-sinr, sinr)
    kap_g = both(gain, gain) * (1.0 / pixels)
    kap_p = both(gain, gain) * (math.sqrt(s) / pixels)
    fr = both(sgain * cosr, sgain * cosr)
    fi = both(-(sgain * sinr), -(sgain * sinr))
    keep = both(keep_h, keep_h)
    sgn = jnp.where(lax.broadcasted_iota(jnp.int32, (1, s), 1) < half, -1.0, 1.0)

    odd = lax.rem(r, 2)
    zq = lax.div(r, 2)
    kq = 2 * odd + w
    row_t = lax.broadcasted_iota(jnp.int32, (th, s), 0)
    tail_r, tail_i = powers(fr, fi, th - row_t, th.bit_length())
    cr, ci = tail_r[0:1], tail_i[0:1]
    row_k = lax.broadcasted_iota(jnp.int32, (8, s), 0)
    in_quad = row_k < 4
    qr, qi = powers(cr, ci, row_k, 3)
    qr, qi = jnp.where(in_quad, qr, 0.0), jnp.where(in_quad, qi, 0.0)
    beyond = jnp.logical_and(in_quad, row_k > kq)
    lr, li = powers(cr, ci, jnp.maximum(row_k - kq - 1, 0), 3)
    lr, li = jnp.where(beyond, lr, 0.0), jnp.where(beyond, li, 0.0)
    rest_r, rest_i = powers(cr, ci, 3 - kq + 0 * row_k, 2)
    c4r, c4i = powers(cr, ci, 4 + 0 * row_k, 3)
    row_z = lax.broadcasted_iota(jnp.int32, (zrecv.shape[0], s), 0)
    far_r, far_i = powers(c4r[0:1], c4i[0:1], row_z, zrecv.shape[0].bit_length())

    ident = jnp.where(
        lax.broadcasted_iota(jnp.int32, (s + 8, s), 0) == lax.broadcasted_iota(jnp.int32, (s + 8, s), 1),
        1.0, 0.0,
    )
    for c in range(CHAINS):
        pall[c * (steps + 1)] = ident
    bquad[...] = jnp.zeros_like(bquad)
    brows[...] = jnp.zeros_like(brows)

    def blank(d, _):
        @pl.when(zq + d >= nz)
        def _():
            zrecv[d - 1] = jnp.zeros(zrecv.shape[1:], F32)

        return 0

    lax.fori_loop(1, zrecv.shape[0] + 1, blank, 0)

    c_mask.wait()
    m_two = both(mfull[own_rows, :], mrem[...]).astype(BF16)
    c_proj.wait()
    pown[...] = (pacc[own_rows, :] + precv[...]) * kap_p
    for cp in copies:
        cp.wait()

    def rows_of(g, _):
        for k in range(2):
            i = 2 * (2 * g + k)
            b0 = bs[pl.ds(i, 2 * nb, stride=s), :]
            b1 = bs[pl.ds(i + 1, 2 * nb, stride=s), :]
            res = jnp.dot(m_two, both(b0, b1).astype(BF16), preferred_element_type=F32)
            gown[pl.ds(pl.multiple_of(i * th, 8), th), :] = res[:, :s]
            gown[pl.ds(pl.multiple_of((i + 1) * th, 8), th), :] = res[:, s:]
        return 0

    lax.fori_loop(0, s // 4, rows_of, 0)

    def step(k, _):
        for c in range(CHAINS):
            t = c * steps + k
            gram = gown[pl.ds(t, s, stride=th), :].astype(BF16)
            p = pall[c * (steps + 1) + k]
            u = p * cosd + turn(p) * sind
            nxt = u - kap_g * jnp.dot(u.astype(BF16), gram, preferred_element_type=F32)
            pall[c * (steps + 1) + k + 1, 0:s, :] = nxt[:s]
            pall[c * (steps + 1) + k + 1, s : s + 8, :] = nxt[s:] + pown[pl.ds(t, 1), :]
        return 0

    lax.fori_loop(0, steps, step, 0)

    def last(c):
        return pall[c * (steps + 1) + steps]

    for p in range(4):
        join(last(2 * p), last(2 * p + 1), comb.at[p])
    join(comb[0], comb[1], comb.at[4])
    join(comb[2], comb[3], comb.at[5])
    join(comb[4], comb[5], mcore)

    c_core = exchange(mcore, mrecv.at[0], 1, partner)
    c_core.start()
    c_core.wait()
    mine = mcore[...]
    theirs = mrecv[0]
    join(jnp.where(w == 0, mine, theirs), jnp.where(w == 0, theirs, mine), mpair)

    c_pair = exchange(mpair, mrecv.at[1], 2, {"roll": r + 1 - 2 * odd, "width": w})
    c_pair.start()
    c_pair.wait()
    mine = mpair[...]
    theirs = mrecv[1]
    join(jnp.where(odd == 0, mine, theirs), jnp.where(odd == 0, theirs, mine), mquad)

    onward = lax.rem(r + 2, n_roll)
    c_x = exchange(xsend, xrecv, 3, {"roll": onward, "width": w})

    @pl.when(r < 2)
    def _():
        xrecv[...] = jnp.broadcast_to(init_ref[...], xrecv.shape)

    @pl.when(r >= 2)
    def _():
        c_x.wait_recv()

    x = xrecv[0:1, :]
    xcol = column(x)

    @pl.when(r < n_roll - 2)
    def _():
        xsend[...] = jnp.broadcast_to(apply(xcol, mquad[...]), xsend.shape)
        c_x.start()

    x = jnp.where(odd == 1, apply(xcol, mrecv[1]), x)
    x = jnp.where(w == 1, apply(column(x), mrecv[0]), x)

    def along(c, xc):
        col = column(xc)
        val = None
        for k in range(steps):
            val = apply(col, pall[c * (steps + 1) + k + 1])
            xs[c * steps + k : c * steps + k + 1, :] = val
        return col, val

    col0, x1 = along(0, x)
    x4 = apply(col0, comb[4])
    x2 = apply(col0, comb[0])
    col4, x5 = along(4, x4)
    x6 = apply(col4, comb[2])
    _, x3 = along(2, x2)
    _, x7 = along(6, x6)
    along(1, x1)
    along(3, x3)
    along(5, x5)
    along(7, x7)

    final = jnp.logical_and(q == nq - 1, row_t == th - 1)
    xf = xs[...]
    v = jnp.where(final, xf, keep * xf)
    ar, ai = fr, fi
    hop = 1
    while hop < th:
        later = jnp.where(row_t < th - hop, pltpu.roll(v, th - hop, 0), 0.0)
        v = v + later * ar + turn(later) * (ai * sgn)
        ar, ai = ar * ar - ai * ai, 2.0 * ar * ai
        hop *= 2

    b_own = v[0:1, :]
    bsend[...] = jnp.broadcast_to(b_own, bsend.shape)

    def quad_copy(e):
        to = lax.rem(kq + e, 4)
        return pltpu.make_async_remote_copy(
            src_ref=bsend, dst_ref=bquad.at[e - 1], send_sem=b_ss.at[e - 1], recv_sem=b_rs.at[e - 1],
            device_id={"roll": 2 * zq + lax.div(to, 2), "width": lax.rem(to, 2)}, device_id_type=MESH,
        )

    trio = [quad_copy(e) for e in (3, 2, 1)]
    for cp in trio:
        cp.start()
    brows[pl.ds(kq, 1), :] = b_own
    for cp in trio:
        cp.wait_recv()
    for e in (1, 2, 3):
        brows[pl.ds(lax.rem(kq - e + 4, 4), 1), :] = bquad[e - 1, 0:1, :]
    bq = brows[...]
    bq_t = turn(bq) * sgn
    zsend[...] = jnp.broadcast_to(jnp.sum(bq * qr + bq_t * qi, axis=0, keepdims=True), zsend.shape)

    def away(d):
        return pltpu.make_async_remote_copy(
            src_ref=zsend, dst_ref=zrecv.at[d - 1], send_sem=z_ss.at[d - 1], recv_sem=z_rs.at[d - 1],
            device_id={"roll": lax.rem(r - 2 * d + n_roll, n_roll), "width": w}, device_id_type=MESH,
        )

    def send_b(d, _):
        @pl.when(zq >= nz - d)
        def _():
            away(nz - d).start()

        return 0

    def recv_b(d, _):
        @pl.when(zq + d < nz)
        def _():
            away(d).wait_recv()

        return 0

    def sent_b(d, _):
        @pl.when(zq >= d)
        def _():
            away(d).wait_send()

        return 0

    lax.fori_loop(1, nz, send_b, 0)
    near = jnp.sum(bq * lr + bq_t * li, axis=0, keepdims=True)
    lax.fori_loop(1, nz, recv_b, 0)
    late = zrecv[:, 0, :]
    s_z = jnp.sum(late * far_r + turn(late) * (far_i * sgn), axis=0, keepdims=True)
    s_z = jnp.broadcast_to(s_z, (8, s))
    s_in = near + s_z * rest_r + turn(s_z) * (rest_i * sgn)
    v = v + s_in[0:1] * tail_r + turn(s_in)[0:1] * (tail_i * sgn)
    ssend[...] = v
    c_s = exchange(ssend, srecv, 4, partner)
    c_s.start()
    out_ref[own_rows, :] = v
    c_s.wait()
    out_ref[oth_rows, :] = srecv[...]

    @pl.when(r < n_roll - 2)
    def _():
        c_x.wait_send()

    for cp in trio:
        cp.wait_send()
    lax.fori_loop(1, nz, sent_b, 0)


def shards(n_roll, lines_y, defect_mask, loading, decay_rate, angle, gain, smooth_gain, initial):
    s = loading.shape[1]
    lines = lines_y.shape[0]
    th = lines // 2
    steps = th // CHAINS
    nb = loading.shape[0] // PIX_BLK
    half = s // 2
    slots = max(8, n_roll // 2)
    vm = pl.BlockSpec(memory_space=pltpu.VMEM)
    smoothed = pl.pallas_call(
        functools.partial(kernel, n_roll),
        out_shape=jax.ShapeDtypeStruct((lines, s), F32),
        in_specs=[pl.BlockSpec(memory_space=pltpu.HBM)] * 8,
        out_specs=vm,
        scratch_shapes=[
            pltpu.VMEM(lines_y.shape, BF16),
            pltpu.VMEM(loading.shape, BF16),
            pltpu.VMEM((nb, lines), jnp.int32),
            pltpu.VMEM((4, 1, half), F32),
            pltpu.VMEM((1, s), F32),
            pltpu.VMEM((lines, nb), F32),
            pltpu.VMEM((th, nb), F32),
            pltpu.VMEM((2 * nb * s, s), F32),
            pltpu.VMEM((s * th, s), F32),
            pltpu.VMEM((lines, s), F32),
            pltpu.VMEM((th, s), F32),
            pltpu.VMEM((th, s), F32),
            pltpu.VMEM((CHAINS * (steps + 1), s + 8, s), F32),
            pltpu.VMEM((6, s + 8, s), F32),
            pltpu.VMEM((s + 8, s), F32),
            pltpu.VMEM((s + 8, s), F32),
            pltpu.VMEM((s + 8, s), F32),
            pltpu.VMEM((2, s + 8, s), F32),
            pltpu.VMEM((th, s), F32),
            pltpu.VMEM((8, s), F32),
            pltpu.VMEM((8, s), F32),
            pltpu.VMEM((8, s), F32),
            pltpu.VMEM((3, 8, s), F32),
            pltpu.VMEM((8, s), F32),
            pltpu.VMEM((8, s), F32),
            pltpu.VMEM((slots, 8, s), F32),
            pltpu.VMEM((th, s), F32),
            pltpu.VMEM((th, s), F32),
            pltpu.SemaphoreType.DMA((2, PIECES)),
            pltpu.SemaphoreType.DMA((6,)),
            pltpu.SemaphoreType.DMA((PIECES,)),
            pltpu.SemaphoreType.DMA((PIECES,)),
            pltpu.SemaphoreType.DMA((6,)),
            pltpu.SemaphoreType.DMA((6,)),
            pltpu.SemaphoreType.DMA((3,)),
            pltpu.SemaphoreType.DMA((3,)),
            pltpu.SemaphoreType.DMA((slots,)),
            pltpu.SemaphoreType.DMA((slots,)),
        ],
        compiler_params=pltpu.CompilerParams(
            collective_id=0, has_side_effects=True, vmem_limit_bytes=60 * 1024 * 1024
        ),
        name="filter_smoother",
    )(
        lines_y, defect_mask.T, loading, decay_rate.reshape(1, half), angle.reshape(1, half),
        gain.reshape(1, half), smooth_gain.reshape(1, half), initial.reshape(1, s),
    )
    image_rows = lax.dot_general(
        smoothed.astype(BF16), loading, (((1,), (1,)), ((), ())), preferred_element_type=F32
    )
    background = (image_rows * (1.0 / math.sqrt(s))).astype(BF16)
    return (smoothed, background)


def solution(mesh):
    in_specs = (
        P(("groups", "roll"), "width"),
        P(("groups", "roll"), "width"),
        P("width", None),
        P(),
        P(),
        P(),
        P(),
        P("groups"),
    )
    out_specs = (P(("groups", "roll"), None), P(("groups", "roll"), "width"))
    return jax.shard_map(
        functools.partial(shards, mesh.shape["roll"]),
        mesh=mesh, in_specs=in_specs, out_specs=out_specs, check_vma=False,
    )
```

```python
import functools
import math

import jax
import jax.numpy as jnp
from jax import lax
from jax.experimental import pallas as pl
from jax.experimental.pallas import tpu as pltpu
from jax.sharding import PartitionSpec as P

PIX_BLK = 128
CHAINS = 8
PIECES = 8
MESH = pl.DeviceIdType.MESH
HI = lax.Precision.HIGHEST
F32 = jnp.float32
BF16 = jnp.bfloat16


def turn(v):
    return pltpu.roll(v, v.shape[-1] // 2, 1)


def join(first, second, dst):
    s = second.shape[1]
    r = jnp.dot(first, second[:s], precision=HI, preferred_element_type=F32)
    dst[0:s, :] = r[:s]
    dst[s : s + 8, :] = r[s:] + second[s:]


def column(x):
    return jnp.broadcast_to(x, (x.shape[1], x.shape[1])).T


def apply(xcol, m):
    s = xcol.shape[0]
    return jnp.sum(m[:s] * xcol, axis=0, keepdims=True) + m[s : s + 1]


def powers(fr, fi, expo, bits):
    tr = jnp.ones(expo.shape, F32)
    ti = jnp.zeros(expo.shape, F32)
    for k in range(bits):
        on = (expo >> k) & 1 == 1
        nr = tr * fr - ti * fi
        ni = tr * fi + ti * fr
        tr = jnp.where(on, nr, tr)
        ti = jnp.where(on, ni, ti)
        fr, fi = fr * fr - fi * fi, 2.0 * fr * fi
    return tr, ti


def kernel(
    n_roll, y_hbm, maskt_hbm, load_hbm, decay_hbm, angle_hbm, gain_hbm, sgain_hbm, init_hbm, out_ref,
    y_ref, load_ref, maskt_ref, par_in, init_ref,
    mfull, mrem, mwide, bs, gown, pacc, precv, pown, pall, comb, mcore, mpair, mquad, mrecv, xs,
    xsend, xrecv, bsend, brecv, ssend, srecv,
    in_s, small_s, g_ss, g_rs, one_ss, one_rs, b_ss, b_rs,
):
    s = load_ref.shape[1]
    half = s // 2
    lines = y_ref.shape[0]
    th = lines // 2
    steps = th // CHAINS
    nb = load_ref.shape[0] // PIX_BLK
    pixels = 2 * load_ref.shape[0]
    nq = 2 * n_roll
    r = lax.axis_index("roll")
    w = lax.axis_index("width")
    q = 2 * r + w
    other = 1 - w
    wide = load_ref.shape[0] // PIECES

    smalls = [
        pltpu.make_async_copy(src, dst, small_s.at[k])
        for k, (src, dst) in enumerate([
            (maskt_hbm, maskt_ref), (decay_hbm, par_in.at[0]), (angle_hbm, par_in.at[1]),
            (gain_hbm, par_in.at[2]), (sgain_hbm, par_in.at[3]), (init_hbm, init_ref),
        ])
    ]
    for cp in smalls:
        cp.start()
    loads = []
    for c in range(PIECES):
        span = pl.ds(c * wide, wide)
        pair = (
            pltpu.make_async_copy(load_hbm.at[span, :], load_ref.at[span, :], in_s.at[0, c]),
            pltpu.make_async_copy(y_hbm.at[:, span], y_ref.at[:, span], in_s.at[1, c]),
        )
        for cp in pair:
            cp.start()
        loads.append(pair)

    def at(place):
        return {"roll": lax.div(place, 2), "width": lax.rem(place, 2)}

    barrier = pltpu.get_barrier_semaphore()

    def greet(d, _):
        pl.semaphore_signal(barrier, inc=1, device_id=at(lax.rem(q + d, nq)), device_id_type=MESH)
        return 0

    lax.fori_loop(1, nq, greet, 0)
    for cp in smalls:
        cp.wait()

    eye = jnp.where(
        lax.broadcasted_iota(jnp.int32, (nb, nb), 0) == lax.broadcasted_iota(jnp.int32, (nb, nb), 1),
        1.0, 0.0,
    ).astype(BF16)
    m_f = lax.dot_general(
        maskt_ref[...].astype(F32).astype(BF16), eye, (((0,), (0,)), ((), ())),
        preferred_element_type=F32,
    )
    mfull[...] = m_f
    m_all = m_f.astype(BF16)

    own_rows = pl.ds(pl.multiple_of(w * th, 8), th)
    oth_rows = pl.ds(pl.multiple_of(other * th, 8), th)

    def exchange(src, dst, k, dev):
        return pltpu.make_async_remote_copy(
            src_ref=src, dst_ref=dst, send_sem=one_ss.at[k], recv_sem=one_rs.at[k],
            device_id=dev, device_id_type=MESH,
        )

    partner = {"roll": r, "width": other}
    c_mask = exchange(mfull.at[oth_rows, :], mrem, 5, partner)

    pacc[...] = jnp.zeros_like(pacc)
    per = 4
    few = nb // PIECES
    copies = []
    for c in range(PIECES):
        for cp in loads[c]:
            cp.wait()

        def blocks(g, _):
            b0 = c * few + g * per
            rows = pl.ds(pl.multiple_of(b0 * PIX_BLK, per * PIX_BLK), per * PIX_BLK)
            hh = load_ref[rows, :]
            for k in range(per):
                h = hh[k * PIX_BLK : (k + 1) * PIX_BLK]
                bs[b0 + k] = lax.dot_general(
                    h, h, (((0,), (0,)), ((), ())), preferred_element_type=F32
                )
            shape = (nb, per * PIX_BLK)
            pick = jnp.where(
                lax.broadcasted_iota(jnp.int32, shape, 0)
                == b0 + lax.broadcasted_iota(jnp.int32, shape, 1) // PIX_BLK,
                1.0, 0.0,
            ).astype(BF16)
            mb = jnp.dot(m_all, pick, preferred_element_type=F32).astype(BF16)
            pacc[...] += jnp.dot(y_ref[:, rows] * mb, hh, preferred_element_type=F32)
            return 0

        lax.fori_loop(0, few // per, blocks, 0)
        if c == 0:
            pl.semaphore_wait(barrier, nq - 1)
            c_mask.start()
        cp = pltpu.make_async_remote_copy(
            src_ref=bs.at[pl.ds(c * few, few)],
            dst_ref=bs.at[pl.ds(nb + c * few, few)],
            send_sem=g_ss.at[c], recv_sem=g_rs.at[c], device_id=partner, device_id_type=MESH,
        )
        cp.start()
        copies.append(cp)

    c_proj = exchange(pacc.at[oth_rows, :], precv, 0, partner)
    c_proj.start()

    decay = par_in[0]
    angle = par_in[1]
    gain = par_in[2]
    sgain = par_in[3]
    radius = 1.0 - decay
    cosr = radius * jnp.cos(angle)
    sinr = radius * jnp.sin(angle)
    keep_h = 1.0 - sgain * radius * radius

    def both(a, b):
        return jnp.concatenate([a, b], axis=1)

    cosd = both(cosr, cosr)
    sind = both(-sinr, sinr)
    kap_g = both(gain, gain) * (1.0 / pixels)
    kap_p = both(gain, gain) * (math.sqrt(s) / pixels)
    fr = both(sgain * cosr, sgain * cosr)
    fi = both(-(sgain * sinr), -(sgain * sinr))
    keep = both(keep_h, keep_h)
    sgn = jnp.where(lax.broadcasted_iota(jnp.int32, (1, s), 1) < half, -1.0, 1.0)

    odd = lax.rem(r, 2)
    row_t = lax.broadcasted_iota(jnp.int32, (th, s), 0)
    tail_r, tail_i = powers(fr, fi, th - row_t, th.bit_length())
    far_r, far_i = powers(
        tail_r[0:1], tail_i[0:1], lax.broadcasted_iota(jnp.int32, (nq, s), 0), nq.bit_length()
    )

    ident = jnp.where(
        lax.broadcasted_iota(jnp.int32, (s + 8, s), 0) == lax.broadcasted_iota(jnp.int32, (s + 8, s), 1),
        1.0, 0.0,
    )
    for c in range(CHAINS):
        pall[c * (steps + 1)] = ident
    brecv[nq - 1] = jnp.zeros(brecv.shape[1:], F32)

    def blank(d, _):
        @pl.when(q + d >= nq)
        def _():
            brecv[d - 1] = jnp.zeros(brecv.shape[1:], F32)

        return 0

    lax.fori_loop(1, nq, blank, 0)

    c_mask.wait()
    m_two = both(mfull[own_rows, :], mrem[...]).astype(BF16)
    spread = jnp.where(
        lax.broadcasted_iota(jnp.int32, (2 * nb, 16 * nb), 0)
        == lax.broadcasted_iota(jnp.int32, (2 * nb, 16 * nb), 1) // 8,
        1.0, 0.0,
    ).astype(BF16)
    m_rep = jnp.dot(m_two, spread, preferred_element_type=F32)
    lane8 = lax.broadcasted_iota(jnp.int32, m_rep.shape, 1) & 7
    for k in range(8):
        mwide[k * th : (k + 1) * th, :] = jnp.where(lane8 == k, m_rep, 0.0).astype(BF16)
    c_proj.wait()
    pown[...] = (pacc[own_rows, :] + precv[...]) * kap_p
    for cp in copies:
        cp.wait()

    def rows_of(g, _):
        i = 16 * g
        wide_b = both(
            bs[:, pl.ds(pl.multiple_of(i, 8), 8), :].reshape(16 * nb, s).astype(BF16),
            bs[:, pl.ds(pl.multiple_of(i + 8, 8), 8), :].reshape(16 * nb, s).astype(BF16),
        )
        res = jnp.dot(mwide[...], wide_b, preferred_element_type=F32)
        gown[pl.ds(pl.multiple_of(i * th, 8), 8 * th), :] = res[:, :s]
        gown[pl.ds(pl.multiple_of((i + 8) * th, 8), 8 * th), :] = res[:, s:]
        return 0

    lax.fori_loop(0, s // 16, rows_of, 0)

    def step(k, _):
        for c in range(CHAINS):
            t = c * steps + k
            gram = gown[pl.ds(t, s, stride=th), :].astype(BF16)
            p = pall[c * (steps + 1) + k]
            u = p * cosd + turn(p) * sind
            nxt = u - kap_g * jnp.dot(u.astype(BF16), gram, preferred_element_type=F32)
            pall[c * (steps + 1) + k + 1, 0:s, :] = nxt[:s]
            pall[c * (steps + 1) + k + 1, s : s + 8, :] = nxt[s:] + pown[pl.ds(t, 1), :]
        return 0

    lax.fori_loop(0, steps, step, 0)

    def last(c):
        return pall[c * (steps + 1) + steps]

    for p in range(4):
        join(last(2 * p), last(2 * p + 1), comb.at[p])
    join(comb[0], comb[1], comb.at[4])
    join(comb[2], comb[3], comb.at[5])
    join(comb[4], comb[5], mcore)

    c_core = exchange(mcore, mrecv.at[0], 1, partner)
    c_core.start()
    c_core.wait()
    mine = mcore[...]
    theirs = mrecv[0]
    join(jnp.where(w == 0, mine, theirs), jnp.where(w == 0, theirs, mine), mpair)

    c_pair = exchange(mpair, mrecv.at[1], 2, {"roll": r + 1 - 2 * odd, "width": w})
    c_pair.start()
    c_pair.wait()
    mine = mpair[...]
    theirs = mrecv[1]
    join(jnp.where(odd == 0, mine, theirs), jnp.where(odd == 0, theirs, mine), mquad)

    onward = lax.rem(r + 2, n_roll)
    c_x = exchange(xsend, xrecv, 3, {"roll": onward, "width": w})

    @pl.when(r < 2)
    def _():
        xrecv[...] = jnp.broadcast_to(init_ref[...], xrecv.shape)

    @pl.when(r >= 2)
    def _():
        c_x.wait_recv()

    x = xrecv[0:1, :]
    xcol = column(x)

    @pl.when(r < n_roll - 2)
    def _():
        xsend[...] = jnp.broadcast_to(apply(xcol, mquad[...]), xsend.shape)
        c_x.start()

    x = jnp.where(odd == 1, apply(xcol, mrecv[1]), x)
    x = jnp.where(w == 1, apply(column(x), mrecv[0]), x)

    def along(c, xc):
        col = column(xc)
        val = None
        for k in range(steps):
            val = apply(col, pall[c * (steps + 1) + k + 1])
            xs[c * steps + k : c * steps + k + 1, :] = val
        return col, val

    col0, x1 = along(0, x)
    x4 = apply(col0, comb[4])
    x2 = apply(col0, comb[0])
    col4, x5 = along(4, x4)
    x6 = apply(col4, comb[2])
    _, x3 = along(2, x2)
    _, x7 = along(6, x6)
    along(1, x1)
    along(3, x3)
    along(5, x5)
    along(7, x7)

    final = jnp.logical_and(q == nq - 1, row_t == th - 1)
    xf = xs[...]
    v = jnp.where(final, xf, keep * xf)
    ar, ai = fr, fi
    hop = 1
    while hop < th:
        later = jnp.where(row_t < th - hop, pltpu.roll(v, th - hop, 0), 0.0)
        v = v + later * ar + turn(later) * (ai * sgn)
        ar, ai = ar * ar - ai * ai, 2.0 * ar * ai
        hop *= 2

    bsend[...] = jnp.broadcast_to(v[0:1, :], bsend.shape)

    def away(d):
        return pltpu.make_async_remote_copy(
            src_ref=bsend, dst_ref=brecv.at[d - 1], send_sem=b_ss.at[d - 1], recv_sem=b_rs.at[d - 1],
            device_id=at(lax.rem(q - d + nq, nq)), device_id_type=MESH,
        )

    def send_b(d, _):
        @pl.when(q >= d)
        def _():
            away(d).start()

        return 0

    def recv_b(d, _):
        @pl.when(q + d < nq)
        def _():
            away(d).wait_recv()

        return 0

    def sent_b(d, _):
        @pl.when(q >= d)
        def _():
            away(d).wait_send()

        return 0

    lax.fori_loop(1, nq, send_b, 0)
    lax.fori_loop(1, nq, recv_b, 0)
    late = brecv[:, 0, :]
    s_in = jnp.sum(late * far_r + turn(late) * (far_i * sgn), axis=0, keepdims=True)
    v = v + s_in * tail_r + turn(jnp.broadcast_to(s_in, (8, s)))[0:1] * (tail_i * sgn)
    ssend[...] = v
    c_s = exchange(ssend, srecv, 4, partner)
    c_s.start()
    out_ref[own_rows, :] = v
    c_s.wait()
    out_ref[oth_rows, :] = srecv[...]

    @pl.when(r < n_roll - 2)
    def _():
        c_x.wait_send()

    lax.fori_loop(1, nq, sent_b, 0)


def shards(n_roll, lines_y, defect_mask, loading, decay_rate, angle, gain, smooth_gain, initial):
    s = loading.shape[1]
    lines = lines_y.shape[0]
    th = lines // 2
    steps = th // CHAINS
    nb = loading.shape[0] // PIX_BLK
    half = s // 2
    nq = 2 * n_roll
    vm = pl.BlockSpec(memory_space=pltpu.VMEM)
    smoothed = pl.pallas_call(
        functools.partial(kernel, n_roll),
        out_shape=jax.ShapeDtypeStruct((lines, s), F32),
        in_specs=[pl.BlockSpec(memory_space=pltpu.HBM)] * 8,
        out_specs=vm,
        scratch_shapes=[
            pltpu.VMEM(lines_y.shape, BF16),
            pltpu.VMEM(loading.shape, BF16),
            pltpu.VMEM((nb, lines), jnp.int32),
            pltpu.VMEM((4, 1, half), F32),
            pltpu.VMEM((1, s), F32),
            pltpu.VMEM((lines, nb), F32),
            pltpu.VMEM((th, nb), F32),
            pltpu.VMEM((8 * th, 16 * nb), BF16),
            pltpu.VMEM((2 * nb, s, s), F32),
            pltpu.VMEM((s * th, s), F32),
            pltpu.VMEM((lines, s), F32),
            pltpu.VMEM((th, s), F32),
            pltpu.VMEM((th, s), F32),
            pltpu.VMEM((CHAINS * (steps + 1), s + 8, s), F32),
            pltpu.VMEM((6, s + 8, s), F32),
            pltpu.VMEM((s + 8, s), F32),
            pltpu.VMEM((s + 8, s), F32),
            pltpu.VMEM((s + 8, s), F32),
            pltpu.VMEM((2, s + 8, s), F32),
            pltpu.VMEM((th, s), F32),
            pltpu.VMEM((8, s), F32),
            pltpu.VMEM((8, s), F32),
            pltpu.VMEM((8, s), F32),
            pltpu.VMEM((nq, 8, s), F32),
            pltpu.VMEM((th, s), F32),
            pltpu.VMEM((th, s), F32),
            pltpu.SemaphoreType.DMA((2, PIECES)),
            pltpu.SemaphoreType.DMA((6,)),
            pltpu.SemaphoreType.DMA((PIECES,)),
            pltpu.SemaphoreType.DMA((PIECES,)),
            pltpu.SemaphoreType.DMA((6,)),
            pltpu.SemaphoreType.DMA((6,)),
            pltpu.SemaphoreType.DMA((nq,)),
            pltpu.SemaphoreType.DMA((nq,)),
        ],
        compiler_params=pltpu.CompilerParams(
            collective_id=0, has_side_effects=True, vmem_limit_bytes=60 * 1024 * 1024
        ),
        name="filter_smoother",
    )(
        lines_y, defect_mask.T, loading, decay_rate.reshape(1, half), angle.reshape(1, half),
        gain.reshape(1, half), smooth_gain.reshape(1, half), initial.reshape(1, s),
    )
    image_rows = lax.dot_general(
        smoothed.astype(BF16), loading, (((1,), (1,)), ((), ())), preferred_element_type=F32
    )
    background = (image_rows * (1.0 / math.sqrt(s))).astype(BF16)
    return (smoothed, background)


def solution(mesh):
    in_specs = (
        P(("groups", "roll"), "width"),
        P(("groups", "roll"), "width"),
        P("width", None),
        P(),
        P(),
        P(),
        P(),
        P("groups"),
    )
    out_specs = (P(("groups", "roll"), None), P(("groups", "roll"), "width"))
    return jax.shard_map(
        functools.partial(shards, mesh.shape["roll"]),
        mesh=mesh, in_specs=in_specs, out_specs=out_specs, check_vma=False,
    )
```

```python
import functools
import math

import jax
import jax.numpy as jnp
from jax import lax
from jax.experimental import pallas as pl
from jax.experimental.pallas import tpu as pltpu
from jax.sharding import PartitionSpec as P

PIX_BLK = 128
CHAINS = 8
PIECES = 8
MESH = pl.DeviceIdType.MESH
HI = lax.Precision.HIGHEST
F32 = jnp.float32
BF16 = jnp.bfloat16


def turn(v):
    return pltpu.roll(v, v.shape[-1] // 2, 1)


def join(first, second, dst):
    s = second.shape[1]
    r = jnp.dot(first, second[:s], precision=HI, preferred_element_type=F32)
    dst[0:s, :] = r[:s]
    dst[s : s + 8, :] = r[s:] + second[s:]


def column(x):
    return jnp.broadcast_to(x, (x.shape[1], x.shape[1])).T


def apply(xcol, m):
    s = xcol.shape[0]
    return jnp.sum(m[:s] * xcol, axis=0, keepdims=True) + m[s : s + 1]


def powers(fr, fi, expo, bits):
    tr = jnp.ones(expo.shape, F32)
    ti = jnp.zeros(expo.shape, F32)
    for k in range(bits):
        on = (expo >> k) & 1 == 1
        nr = tr * fr - ti * fi
        ni = tr * fi + ti * fr
        tr = jnp.where(on, nr, tr)
        ti = jnp.where(on, ni, ti)
        fr, fi = fr * fr - fi * fi, 2.0 * fr * fi
    return tr, ti


def kernel(
    n_roll, y_hbm, maskt_hbm, load_hbm, decay_hbm, angle_hbm, gain_hbm, sgain_hbm, init_hbm, out_ref,
    y_ref, load_ref, maskt_ref, par_in, init_ref,
    mfull, mrem, mwide, bs, gown, pacc, precv, pown, pall, comb, mcore, mpair, mquad, mrecv, xs,
    xsend, xrecv, bsend, brecv, ssend, srecv,
    in_s, small_s, g_ss, g_rs, one_ss, one_rs, b_ss, b_rs,
):
    s = load_ref.shape[1]
    half = s // 2
    lines = y_ref.shape[0]
    th = lines // 2
    steps = th // CHAINS
    nb = load_ref.shape[0] // PIX_BLK
    pixels = 2 * load_ref.shape[0]
    nq = 2 * n_roll
    r = lax.axis_index("roll")
    w = lax.axis_index("width")
    q = 2 * r + w
    other = 1 - w
    wide = load_ref.shape[0] // PIECES

    smalls = [
        pltpu.make_async_copy(src, dst, small_s.at[k])
        for k, (src, dst) in enumerate([
            (maskt_hbm, maskt_ref), (decay_hbm, par_in.at[0]), (angle_hbm, par_in.at[1]),
            (gain_hbm, par_in.at[2]), (sgain_hbm, par_in.at[3]), (init_hbm, init_ref),
        ])
    ]
    for cp in smalls:
        cp.start()
    loads = []
    for c in range(PIECES):
        span = pl.ds(c * wide, wide)
        pair = (
            pltpu.make_async_copy(load_hbm.at[span, :], load_ref.at[span, :], in_s.at[0, c]),
            pltpu.make_async_copy(y_hbm.at[:, span], y_ref.at[:, span], in_s.at[1, c]),
        )
        for cp in pair:
            cp.start()
        loads.append(pair)

    def at(place):
        return {"roll": lax.div(place, 2), "width": lax.rem(place, 2)}

    barrier = pltpu.get_barrier_semaphore()

    def greet(roll, width):
        pl.semaphore_signal(
            barrier, inc=1, device_id={"roll": roll, "width": width}, device_id_type=MESH
        )

    greet(r, other)
    greet(r + 1 - 2 * lax.rem(r, 2), w)

    @pl.when(r >= 2)
    def _():
        greet(r - 2, w)

    @pl.when(r < n_roll - 2)
    def _():
        greet(r + 2, w)

    for cp in smalls:
        cp.wait()

    eye = jnp.where(
        lax.broadcasted_iota(jnp.int32, (nb, nb), 0) == lax.broadcasted_iota(jnp.int32, (nb, nb), 1),
        1.0, 0.0,
    ).astype(BF16)
    m_f = lax.dot_general(
        maskt_ref[...].astype(F32).astype(BF16), eye, (((0,), (0,)), ((), ())),
        preferred_element_type=F32,
    )
    mfull[...] = m_f
    m_all = m_f.astype(BF16)

    own_rows = pl.ds(pl.multiple_of(w * th, 8), th)
    oth_rows = pl.ds(pl.multiple_of(other * th, 8), th)

    def exchange(src, dst, k, dev):
        return pltpu.make_async_remote_copy(
            src_ref=src, dst_ref=dst, send_sem=one_ss.at[k], recv_sem=one_rs.at[k],
            device_id=dev, device_id_type=MESH,
        )

    partner = {"roll": r, "width": other}
    c_mask = exchange(mfull.at[oth_rows, :], mrem, 5, partner)

    pacc[...] = jnp.zeros_like(pacc)
    per = 4
    few = nb // PIECES
    copies = []
    for c in range(PIECES):
        for cp in loads[c]:
            cp.wait()

        def blocks(g, _):
            b0 = c * few + g * per
            rows = pl.ds(pl.multiple_of(b0 * PIX_BLK, per * PIX_BLK), per * PIX_BLK)
            hh = load_ref[rows, :]
            for k in range(per):
                h = hh[k * PIX_BLK : (k + 1) * PIX_BLK]
                bs[b0 + k] = lax.dot_general(
                    h, h, (((0,), (0,)), ((), ())), preferred_element_type=F32
                )
            shape = (nb, per * PIX_BLK)
            pick = jnp.where(
                lax.broadcasted_iota(jnp.int32, shape, 0)
                == b0 + lax.broadcasted_iota(jnp.int32, shape, 1) // PIX_BLK,
                1.0, 0.0,
            ).astype(BF16)
            mb = jnp.dot(m_all, pick, preferred_element_type=F32).astype(BF16)
            pacc[...] += jnp.dot(y_ref[:, rows] * mb, hh, preferred_element_type=F32)
            return 0

        lax.fori_loop(0, few // per, blocks, 0)
        if c == 0:
            peers = 2 + jnp.where(r >= 2, 1, 0) + jnp.where(r < n_roll - 2, 1, 0)
            pl.semaphore_wait(barrier, peers)
            c_mask.start()
        cp = pltpu.make_async_remote_copy(
            src_ref=bs.at[pl.ds(c * few, few)],
            dst_ref=bs.at[pl.ds(nb + c * few, few)],
            send_sem=g_ss.at[c], recv_sem=g_rs.at[c], device_id=partner, device_id_type=MESH,
        )
        cp.start()
        copies.append(cp)

    c_proj = exchange(pacc.at[oth_rows, :], precv, 0, partner)
    c_proj.start()

    decay = par_in[0]
    angle = par_in[1]
    gain = par_in[2]
    sgain = par_in[3]
    radius = 1.0 - decay
    cosr = radius * jnp.cos(angle)
    sinr = radius * jnp.sin(angle)
    keep_h = 1.0 - sgain * radius * radius

    def both(a, b):
        return jnp.concatenate([a, b], axis=1)

    cosd = both(cosr, cosr)
    sind = both(-sinr, sinr)
    kap_g = both(gain, gain) * (1.0 / pixels)
    kap_p = both(gain, gain) * (math.sqrt(s) / pixels)
    fr = both(sgain * cosr, sgain * cosr)
    fi = both(-(sgain * sinr), -(sgain * sinr))
    keep = both(keep_h, keep_h)
    sgn = jnp.where(lax.broadcasted_iota(jnp.int32, (1, s), 1) < half, -1.0, 1.0)

    odd = lax.rem(r, 2)
    row_t = lax.broadcasted_iota(jnp.int32, (th, s), 0)
    tail_r, tail_i = powers(fr, fi, th - row_t, th.bit_length())
    far_r, far_i = powers(
        tail_r[0:1], tail_i[0:1], lax.broadcasted_iota(jnp.int32, (nq, s), 0), nq.bit_length()
    )

    ident = jnp.where(
        lax.broadcasted_iota(jnp.int32, (s + 8, s), 0) == lax.broadcasted_iota(jnp.int32, (s + 8, s), 1),
        1.0, 0.0,
    )
    for c in range(CHAINS):
        pall[c * (steps + 1)] = ident
    brecv[nq - 1] = jnp.zeros(brecv.shape[1:], F32)

    def blank(d, _):
        @pl.when(q + d >= nq)
        def _():
            brecv[d - 1] = jnp.zeros(brecv.shape[1:], F32)

        return 0

    lax.fori_loop(1, nq, blank, 0)

    c_mask.wait()
    m_two = both(mfull[own_rows, :], mrem[...]).astype(BF16)
    spread = jnp.where(
        lax.broadcasted_iota(jnp.int32, (2 * nb, 16 * nb), 0)
        == lax.broadcasted_iota(jnp.int32, (2 * nb, 16 * nb), 1) // 8,
        1.0, 0.0,
    ).astype(BF16)
    m_rep = jnp.dot(m_two, spread, preferred_element_type=F32)
    lane8 = lax.broadcasted_iota(jnp.int32, m_rep.shape, 1) & 7
    for k in range(8):
        mwide[k * th : (k + 1) * th, :] = jnp.where(lane8 == k, m_rep, 0.0).astype(BF16)
    c_proj.wait()
    pown[...] = (pacc[own_rows, :] + precv[...]) * kap_p
    for cp in copies:
        cp.wait()

    def rows_of(g, _):
        i = 16 * g
        wide_b = both(
            bs[:, pl.ds(pl.multiple_of(i, 8), 8), :].reshape(16 * nb, s).astype(BF16),
            bs[:, pl.ds(pl.multiple_of(i + 8, 8), 8), :].reshape(16 * nb, s).astype(BF16),
        )
        res = jnp.dot(mwide[...], wide_b, preferred_element_type=F32)
        gown[pl.ds(pl.multiple_of(i * th, 8), 8 * th), :] = res[:, :s]
        gown[pl.ds(pl.multiple_of((i + 8) * th, 8), 8 * th), :] = res[:, s:]
        return 0

    lax.fori_loop(0, s // 16, rows_of, 0)

    def step(k, _):
        for c in range(CHAINS):
            t = c * steps + k
            gram = gown[pl.ds(t, s, stride=th), :].astype(BF16)
            p = pall[c * (steps + 1) + k]
            u = p * cosd + turn(p) * sind
            nxt = u - kap_g * jnp.dot(u.astype(BF16), gram, preferred_element_type=F32)
            pall[c * (steps + 1) + k + 1, 0:s, :] = nxt[:s]
            pall[c * (steps + 1) + k + 1, s : s + 8, :] = nxt[s:] + pown[pl.ds(t, 1), :]
        return 0

    lax.fori_loop(0, steps, step, 0)

    def last(c):
        return pall[c * (steps + 1) + steps]

    for p in range(4):
        join(last(2 * p), last(2 * p + 1), comb.at[p])
    join(comb[0], comb[1], comb.at[4])
    join(comb[2], comb[3], comb.at[5])
    join(comb[4], comb[5], mcore)

    c_core = exchange(mcore, mrecv.at[0], 1, partner)
    c_core.start()
    c_core.wait()
    mine = mcore[...]
    theirs = mrecv[0]
    join(jnp.where(w == 0, mine, theirs), jnp.where(w == 0, theirs, mine), mpair)

    c_pair = exchange(mpair, mrecv.at[1], 2, {"roll": r + 1 - 2 * odd, "width": w})
    c_pair.start()
    c_pair.wait()
    mine = mpair[...]
    theirs = mrecv[1]
    join(jnp.where(odd == 0, mine, theirs), jnp.where(odd == 0, theirs, mine), mquad)

    onward = lax.rem(r + 2, n_roll)
    c_x = exchange(xsend, xrecv, 3, {"roll": onward, "width": w})

    @pl.when(r < 2)
    def _():
        xrecv[...] = jnp.broadcast_to(init_ref[...], xrecv.shape)

    @pl.when(r >= 2)
    def _():
        c_x.wait_recv()

    x = xrecv[0:1, :]
    xcol = column(x)

    @pl.when(r < n_roll - 2)
    def _():
        xsend[...] = jnp.broadcast_to(apply(xcol, mquad[...]), xsend.shape)
        c_x.start()

    x = jnp.where(odd == 1, apply(xcol, mrecv[1]), x)
    x = jnp.where(w == 1, apply(column(x), mrecv[0]), x)

    def along(c, xc):
        col = column(xc)
        val = None
        for k in range(steps):
            val = apply(col, pall[c * (steps + 1) + k + 1])
            xs[c * steps + k : c * steps + k + 1, :] = val
        return col, val

    col0, x1 = along(0, x)
    x4 = apply(col0, comb[4])
    x2 = apply(col0, comb[0])
    col4, x5 = along(4, x4)
    x6 = apply(col4, comb[2])
    _, x3 = along(2, x2)
    _, x7 = along(6, x6)
    along(1, x1)
    along(3, x3)
    along(5, x5)
    along(7, x7)

    final = jnp.logical_and(q == nq - 1, row_t == th - 1)
    xf = xs[...]
    v = jnp.where(final, xf, keep * xf)
    ar, ai = fr, fi
    hop = 1
    while hop < th:
        later = jnp.where(row_t < th - hop, pltpu.roll(v, th - hop, 0), 0.0)
        v = v + later * ar + turn(later) * (ai * sgn)
        ar, ai = ar * ar - ai * ai, 2.0 * ar * ai
        hop *= 2

    bsend[...] = jnp.broadcast_to(v[0:1, :], bsend.shape)

    def away(d):
        return pltpu.make_async_remote_copy(
            src_ref=bsend, dst_ref=brecv.at[d - 1], send_sem=b_ss.at[d - 1], recv_sem=b_rs.at[d - 1],
            device_id=at(lax.rem(q - d + nq, nq)), device_id_type=MESH,
        )

    def send_b(d, _):
        @pl.when(q >= d)
        def _():
            away(d).start()

        return 0

    def recv_b(d, _):
        @pl.when(q + d < nq)
        def _():
            away(d).wait_recv()

        return 0

    def sent_b(d, _):
        @pl.when(q >= d)
        def _():
            away(d).wait_send()

        return 0

    lax.fori_loop(1, nq, send_b, 0)
    lax.fori_loop(1, nq, recv_b, 0)
    late = brecv[:, 0, :]
    s_in = jnp.sum(late * far_r + turn(late) * (far_i * sgn), axis=0, keepdims=True)
    v = v + s_in * tail_r + turn(jnp.broadcast_to(s_in, (8, s)))[0:1] * (tail_i * sgn)
    ssend[...] = v
    c_s = exchange(ssend, srecv, 4, partner)
    c_s.start()
    out_ref[own_rows, :] = v
    c_s.wait()
    out_ref[oth_rows, :] = srecv[...]

    @pl.when(r < n_roll - 2)
    def _():
        c_x.wait_send()

    lax.fori_loop(1, nq, sent_b, 0)


def shards(n_roll, lines_y, defect_mask, loading, decay_rate, angle, gain, smooth_gain, initial):
    s = loading.shape[1]
    lines = lines_y.shape[0]
    th = lines // 2
    steps = th // CHAINS
    nb = loading.shape[0] // PIX_BLK
    half = s // 2
    nq = 2 * n_roll
    vm = pl.BlockSpec(memory_space=pltpu.VMEM)
    smoothed = pl.pallas_call(
        functools.partial(kernel, n_roll),
        out_shape=jax.ShapeDtypeStruct((lines, s), F32),
        in_specs=[pl.BlockSpec(memory_space=pltpu.HBM)] * 8,
        out_specs=vm,
        scratch_shapes=[
            pltpu.VMEM(lines_y.shape, BF16),
            pltpu.VMEM(loading.shape, BF16),
            pltpu.VMEM((nb, lines), jnp.int32),
            pltpu.VMEM((4, 1, half), F32),
            pltpu.VMEM((1, s), F32),
            pltpu.VMEM((lines, nb), F32),
            pltpu.VMEM((th, nb), F32),
            pltpu.VMEM((8 * th, 16 * nb), BF16),
            pltpu.VMEM((2 * nb, s, s), F32),
            pltpu.VMEM((s * th, s), F32),
            pltpu.VMEM((lines, s), F32),
            pltpu.VMEM((th, s), F32),
            pltpu.VMEM((th, s), F32),
            pltpu.VMEM((CHAINS * (steps + 1), s + 8, s), F32),
            pltpu.VMEM((6, s + 8, s), F32),
            pltpu.VMEM((s + 8, s), F32),
            pltpu.VMEM((s + 8, s), F32),
            pltpu.VMEM((s + 8, s), F32),
            pltpu.VMEM((2, s + 8, s), F32),
            pltpu.VMEM((th, s), F32),
            pltpu.VMEM((8, s), F32),
            pltpu.VMEM((8, s), F32),
            pltpu.VMEM((8, s), F32),
            pltpu.VMEM((nq, 8, s), F32),
            pltpu.VMEM((th, s), F32),
            pltpu.VMEM((th, s), F32),
            pltpu.SemaphoreType.DMA((2, PIECES)),
            pltpu.SemaphoreType.DMA((6,)),
            pltpu.SemaphoreType.DMA((PIECES,)),
            pltpu.SemaphoreType.DMA((PIECES,)),
            pltpu.SemaphoreType.DMA((6,)),
            pltpu.SemaphoreType.DMA((6,)),
            pltpu.SemaphoreType.DMA((nq,)),
            pltpu.SemaphoreType.DMA((nq,)),
        ],
        compiler_params=pltpu.CompilerParams(
            collective_id=0, has_side_effects=True, vmem_limit_bytes=60 * 1024 * 1024
        ),
        name="filter_smoother",
    )(
        lines_y, defect_mask.T, loading, decay_rate.reshape(1, half), angle.reshape(1, half),
        gain.reshape(1, half), smooth_gain.reshape(1, half), initial.reshape(1, s),
    )
    image_rows = lax.dot_general(
        smoothed.astype(BF16), loading, (((1,), (1,)), ((), ())), preferred_element_type=F32
    )
    background = (image_rows * (1.0 / math.sqrt(s))).astype(BF16)
    return (smoothed, background)


def solution(mesh):
    in_specs = (
        P(("groups", "roll"), "width"),
        P(("groups", "roll"), "width"),
        P("width", None),
        P(),
        P(),
        P(),
        P(),
        P("groups"),
    )
    out_specs = (P(("groups", "roll"), None), P(("groups", "roll"), "width"))
    return jax.shard_map(
        functools.partial(shards, mesh.shape["roll"]),
        mesh=mesh, in_specs=in_specs, out_specs=out_specs, check_vma=False,
    )
```
